512 devices in a mesh: grp: 16 (over x_lo, z), fsdp: 32 (over y, x_hi, core).
Axes of the slice: x: 4 (x_hi: 2, x_lo: 2; x = x_hi * 2 + x_lo), y: 8, z: 8, core: 2. Of those that a mesh axis runs over, the one named last changes fastest.
Arguments:
- weight: float32 [16, 4608, 256], P('grp', 'fsdp'), may hold values from -6 to 6
- momentum: float32 [16, 4608, 256], P('grp', 'fsdp'), may hold values from -4 to 4
- adam_mean: float32 [16, 4608, 256], P('grp', 'fsdp'), may hold values from -0.00048828125 to 0.00048828125
- adam_var: float32 [16, 4608, 256], P('grp', 'fsdp'), may hold values from 1.0007694e-09 to 1.0007693e-08
- inputs: bfloat16 [16, 8192, 4608], P('grp', 'fsdp'), may hold values from -6 to 6
- targets: bfloat16 [16, 8192, 256], P('grp', 'fsdp'), may hold values from -6 to 6
- states: bfloat16 [16, 4096, 4608], P('grp', 'fsdp'), may hold values from -6 to 6
- partner: int32 [16, 32], P(None, 'fsdp'), may hold values from 0 to 15, as said below
Outputs:
- new_weight: float32 [16, 4608, 256], P('grp', 'fsdp')
- new_momentum: float32 [16, 4608, 256], P('grp', 'fsdp')
- rollout_keys: bfloat16 [16, 4096, 256], P('grp', 'fsdp')
The draws below stay inside these ranges and needn't reach their ends.
Inputs may be any that keep to these rules, and one draw needn't show every extreme that they name: For each row block f, partner[:, f] pairs the groups: partner[g, f] != g and partner[partner[g, f], f] = g.
All inputs are finite; a program needn't handle non-finite values.
Results may differ from the reference program's by a relative error of at most 0.005.
Values may be sent and summed in bfloat16 or wider, within the bound.
No kernel may reach another device: no remote copies, remote signals or barrier semaphores. Data moves between devices by JAX's collectives and lax.ppermute only.
A program may use at most 64 MiB of HBM per device.

```python
import math
import jax
import jax.numpy as jnp
from jax import lax

D = 4608
KW = 256
TOK_DEV = 256
TOKENS = 8192
PRE = 4096
N_GRP = 16
N_FSDP = 32


def one_pairing(key):
    order = jax.random.permutation(key, N_GRP).astype(jnp.int32)
    first = order[0::2]
    second = order[1::2]
    mates = jnp.zeros((N_GRP,), jnp.int32)
    return mates.at[first].set(second).at[second].set(first)


def draw_partner(key, part):
    keys = jax.random.split(jax.random.fold_in(key, 7), N_FSDP)
    return jnp.transpose(jax.vmap(one_pairing)(keys)).astype(jnp.int32)


def spiked(values, key, source, target, blocks, factor):
    def block_of(axis_at):
        return (jnp.arange(values.shape[axis_at]) // (values.shape[axis_at] // blocks)).reshape((-1,) + (1,) * (values.ndim - 1 - axis_at))

    near = jax.random.permutation(key, blocks)[block_of(target)]
    other_side = (block_of(target) + blocks // 2) % blocks
    return jnp.where((block_of(source) == near) | (block_of(source) == other_side), factor * values, values)


def levels(key, shape, pieces, low, top_value):
    def one(dim, blocks):
        heights = jax.random.uniform(jax.random.fold_in(jax.random.fold_in(key, 6), dim), (blocks,), jnp.float32, low / len(pieces), top_value / len(pieces))
        return jnp.repeat(jnp.exp(heights), shape[dim] // blocks).reshape((-1,) + (1,) * (len(shape) - dim - 1))

    level = one(*pieces[0])
    for cut in pieces[1:]:
        level = level * one(*cut)
    return level


def centred(stream_key, dims, scale, bound, shards=(), held_as=jnp.bfloat16):
    result = jax.random.normal(stream_key, dims, jnp.float32) * scale
    if len(shards) > 0:
        result = levels(stream_key, dims, shards, -0.22, 0.18) * result
    return jnp.clip(result, min=-bound, max=bound).astype(held_as)


def noise_with(own_key, shape, width, reach, pieces, heavy, dtype=jnp.bfloat16):
    values = width * jax.random.normal(own_key, shape, jnp.float32)
    if pieces:
        values = values * levels(own_key, shape, pieces, -0.22, 0.18)
    return jnp.clip(spiked(values, jax.random.fold_in(own_key, 3), *heavy), -reach, reach).astype(dtype)


def setup_inputs(seed: int = 0) -> dict:
    key_of = jax.random.split(jax.random.key(seed), 9)
    weight = centred(key_of[0], (N_GRP, D, KW), 1.0, 6.0, ((0, 16), (1, 32)), jnp.float32)
    momentum = centred(key_of[1], (N_GRP, D, KW), 0.25, 4.0, ((0, 16), (1, 32)), jnp.float32)
    adam_mean = centred(key_of[2], (N_GRP, D, KW), (0.1 * (D ** -2 + 2 * (TOKENS * D) ** -1) ** 0.5), 0.00048828125, ((0, 16), (1, 32)), jnp.float32)
    adam_var = jnp.clip(jnp.exp(math.log(1.0007693340696733e-08) - 2.3025851 * jax.random.uniform(key_of[3], (N_GRP, D, KW), jnp.float32) ** levels(key_of[3], (N_GRP, D, KW), ((0, 16), (1, 32)), -0.2, 0.2)), 1.0007693562741338e-09, 1.0007693340696733e-08)
    inputs = noise_with(key_of[4], (N_GRP, TOKENS, D), 1.0, 6.0, ((0, 16), (1, 32)), (1, 2, 32, 2.75))
    targets = centred(key_of[5], (N_GRP, TOKENS, KW), 1.0, 6.0, ((0, 16), (1, 32)))
    states = centred(key_of[6], (N_GRP, PRE, D), 1.0, 6.0, ((0, 16), (1, 32)))
    partner = draw_partner(jax.random.fold_in(key_of[8], 71), 0)
    return {"weight": weight, "momentum": momentum, "adam_mean": adam_mean, "adam_var": adam_var, "inputs": inputs, "targets": targets, "states": states, "partner": partner}


beta_one = 0.9
beta_two = 0.95
adam_eps = 1e-08
inner_rate = 0.1
decay_rate = 0.1
bias_one = 1.0 - (0.9 ** 50) ** 2
bias_two = 1.0 - (0.95 ** 50) ** 2
outer_rate = 0.7
outer_beta = 0.9

def group_delta(operands):
    weight, mean, var, inputs, targets = operands
    scale = 1.0 / math.sqrt(D)
    weight_bf = weight.astype(jnp.bfloat16)
    pred = jnp.dot(inputs, weight_bf, preferred_element_type=jnp.float32) * scale
    resid = ((pred - targets.astype(jnp.float32)) / TOKENS).astype(jnp.bfloat16)
    blocks_in = inputs.reshape(N_FSDP, TOK_DEV, D).astype(jnp.float32)
    blocks_res = resid.reshape(N_FSDP, TOK_DEV, KW).astype(jnp.float32)
    partial_sums = jnp.einsum('btd,btc->bdc', blocks_in, blocks_res)
    rounded = lax.optimization_barrier(partial_sums.astype(jnp.bfloat16)).astype(jnp.float32)
    grad = lax.optimization_barrier(jnp.sum(rounded, axis=0)) * scale
    mean_new = beta_one * mean + (1.0 - beta_one) * grad
    var_new = beta_two * var + (1.0 - beta_two) * grad * grad
    update = mean_new / bias_one / (jnp.sqrt(var_new / bias_two) + adam_eps) + decay_rate * weight
    return inner_rate * update

def group_keys(operands):
    states, weight_bf = operands
    scale = 1.0 / math.sqrt(D)
    keys = jnp.dot(states, weight_bf, preferred_element_type=jnp.float32) * scale
    return keys.astype(jnp.bfloat16)

def reference(weight, momentum, adam_mean, adam_var, inputs, targets, states, partner):
    delta = lax.map(group_delta, (weight, adam_mean, adam_var, inputs, targets))
    blocked = delta.reshape(N_GRP, N_FSDP, D // N_FSDP, KW)
    index = jnp.broadcast_to(partner.astype(jnp.int32)[:, :, None, None], blocked.shape)
    partner_delta = jnp.take_along_axis(blocked, index, axis=0).reshape(N_GRP, D, KW)
    average = 0.5 * (delta + partner_delta)
    new_momentum = outer_beta * momentum + average
    new_weight = weight - outer_rate * (average + outer_beta * new_momentum)
    rollout_keys = lax.map(group_keys, (states, new_weight.astype(jnp.bfloat16)))
    return (new_weight, new_momentum, rollout_keys)
```

```python
import math

import jax
import jax.numpy as jnp
from jax import lax
from jax.sharding import Mesh
from jax.sharding import PartitionSpec as P

D = 4608

beta_one = 0.9
beta_two = 0.95
adam_eps = 1e-08
inner_rate = 0.1
decay_rate = 0.1
bias_one = 1.0 - (0.9**50) ** 2
bias_two = 1.0 - (0.95**50) ** 2
outer_rate = 0.7
outer_beta = 0.9

GRP = ("xl", "z")
CHIPS = ("y", "xh")
SWAP = [(0, 1), (1, 0)]


def spread_all(block, axes, n):
    return lax.all_to_all(jnp.broadcast_to(block[None], (n,) + block.shape), axes, 0, 0)


def by_core(mine, other):
    core = lax.axis_index("c")
    return jnp.stack([jnp.where(core == 0, mine, other), jnp.where(core == 0, other, mine)], axis=1)


def gather_rows(block, chips):
    mine = spread_all(block, CHIPS, chips)
    other = lax.ppermute(mine, "c", SWAP)
    return by_core(mine, other).reshape(-1, block.shape[1])


def shards(weight, momentum, adam_mean, adam_var, inputs, targets, states, partner):
    scale = 1.0 / math.sqrt(D)
    chips = lax.axis_size("y") * lax.axis_size("xh")
    groups = lax.axis_size("xl") * lax.axis_size("z")
    core = lax.axis_index("c")
    weight_loc = weight[0]
    rows, width = weight_loc.shape
    inputs_loc = inputs[0]
    tokens_all = inputs_loc.shape[0] * chips * 2
    full = gather_rows(weight_loc.astype(jnp.bfloat16), chips)
    pred = jnp.dot(inputs_loc, full, preferred_element_type=jnp.float32) * scale
    resid = ((pred - targets[0].astype(jnp.float32)) / tokens_all).astype(jnp.bfloat16)
    part = lax.dot_general(
        inputs_loc, resid, (((0,), (0,)), ((), ())), preferred_element_type=jnp.float32
    ).reshape(chips, 2, rows, width)
    keep = jnp.where(core == 0, part[:, 0], part[:, 1])
    send = jnp.where(core == 0, part[:, 1], part[:, 0]).astype(jnp.bfloat16)
    both = (keep + lax.ppermute(send, "c", SWAP).astype(jnp.float32)).astype(jnp.bfloat16)
    pieces = lax.all_to_all(both, CHIPS, 0, 0)
    grad = jnp.sum(pieces.astype(jnp.float32), axis=0) * scale
    mean_new = beta_one * adam_mean[0] + (1.0 - beta_one) * grad
    var_new = beta_two * adam_var[0] + (1.0 - beta_two) * grad * grad
    update = (
        mean_new / bias_one / (jnp.sqrt(var_new / bias_two) + adam_eps) + decay_rate * weight_loc
    )
    delta = inner_rate * update
    every = spread_all(delta.astype(jnp.bfloat16), GRP, groups)
    mate = partner[:, 0][lax.axis_index(GRP)]
    partner_delta = lax.dynamic_index_in_dim(every, mate, 0, keepdims=False).astype(jnp.float32)
    average = 0.5 * (delta + partner_delta)
    new_momentum = outer_beta * momentum[0] + average
    new_weight = weight_loc - outer_rate * (average + outer_beta * new_momentum)
    full = gather_rows(new_weight.astype(jnp.bfloat16), chips)
    rollout = jnp.dot(states[0], full, preferred_element_type=jnp.float32) * scale
    return (new_weight[None], new_momentum[None], rollout.astype(jnp.bfloat16)[None])


def solution(mesh):
    fine = Mesh(mesh.devices.reshape(2, 8, 8, 2, 2), ("xl", "z", "y", "xh", "c"))
    grp, fsdp = ("xl", "z"), ("y", "xh", "c")
    row = P(grp, fsdp, None)
    return jax.shard_map(
        shards,
        mesh=fine,
        in_specs=(row, row, row, row, row, row, row, P(None, fsdp)),
        out_specs=(row, row, row),
        check_vma=False,
    )
```

```python
import functools
import math

import jax
import jax.numpy as jnp
from jax import lax
from jax.experimental import pallas as pl
from jax.experimental.pallas import tpu as pltpu
from jax.sharding import Mesh
from jax.sharding import PartitionSpec as P

D = 4608

beta_one = 0.9
beta_two = 0.95
adam_eps = 1e-08
inner_rate = 0.1
decay_rate = 0.1
bias_one = 1.0 - (0.9**50) ** 2
bias_two = 1.0 - (0.95**50) ** 2
outer_rate = 0.7
outer_beta = 0.9
scale = 1.0 / math.sqrt(D)

f32, bf16 = jnp.float32, jnp.bfloat16

AXES = (("xl", 2), ("z", 8), ("yh", 4), ("yl", 2), ("xh", 2), ("c", 2))
GRP = ("xl", "z")
FSDP = ("yh", "yl", "xh", "c")
FAR = ("yh",)
NEAR = ("yl", "xh")
NFAR, NNEAR = 4, 4
GROUPS = 16
SUB = 16
SWAP = [(0, 1), (1, 0)]

VMEM = pl.BlockSpec(memory_space=pltpu.MemorySpace.VMEM)
SMEM = pl.BlockSpec(memory_space=pltpu.MemorySpace.SMEM)


def block_rows(far, near, core, rows):
    start = rows * (2 * NNEAR * far + 2 * near) + rows * core
    return pl.ds(pl.multiple_of(start, 16), rows)


def pred_kernel(mine_ref, other_ref, weight_ref, target_ref, out_ref, full_ref):
    core = lax.axis_index("c")
    rows = weight_ref.shape[2]
    for far in range(NFAR):
        for near in range(NNEAR):
            full_ref[block_rows(far, near, core, rows), :] = weight_ref[near, far]
            full_ref[block_rows(far, near, 1 - core, rows), :] = jnp.zeros_like(weight_ref[near, far])
    mine = jnp.dot(mine_ref[...], full_ref[...], preferred_element_type=f32)
    out_ref[0] = mine * scale - target_ref[...].astype(f32)
    other = jnp.dot(other_ref[...], full_ref[...], preferred_element_type=f32)
    out_ref[1] = other * scale


def grad_kernel(tokens, mine_ref, other_ref, here_ref, there_ref, out_ref, part_ref):
    core = lax.axis_index("c")
    rows = out_ref.shape[2]
    resid_mine = ((here_ref[0] + there_ref[1]) / tokens).astype(bf16)
    resid_other = ((here_ref[1] + there_ref[0]) / tokens).astype(bf16)
    dims = (((0,), (0,)), ((), ()))
    span = 2 * NNEAR * rows
    for far in range(NFAR):
        cols = pl.ds(far * span, span)
        part_ref[far] = lax.dot_general(
            mine_ref[:, cols], resid_mine, dims, preferred_element_type=f32
        ) + lax.dot_general(other_ref[:, cols], resid_other, dims, preferred_element_type=f32)
        for near in range(NNEAR):
            out_ref[near, far] = part_ref[far, block_rows(0, near, core, rows), :].astype(bf16)


def sum_kernel(parts_ref, out_ref):
    total = parts_ref[0].astype(f32)
    for i in range(1, NNEAR):
        total += parts_ref[i].astype(f32)
    out_ref[...] = total.astype(bf16)


def delta_kernel(parts_ref, weight_ref, mean_ref, var_ref, delta_ref, pieces_ref):
    total = parts_ref[0].astype(f32)
    for i in range(1, NFAR):
        total += parts_ref[i].astype(f32)
    grad = total * scale
    mean_new = beta_one * mean_ref[...] + (1.0 - beta_one) * grad
    var_new = beta_two * var_ref[...] + (1.0 - beta_two) * grad * grad
    update = mean_new / bias_one / (jnp.sqrt(var_new / bias_two) + adam_eps)
    delta = inner_rate * (update + decay_rate * weight_ref[...])
    delta_ref[...] = delta
    rows = delta.shape[0]
    for i in range(GROUPS):
        if (i + 1) * SUB <= rows:
            pieces_ref[i] = delta[i * SUB : (i + 1) * SUB].astype(bf16)
        else:
            pieces_ref[i] = jnp.zeros_like(pieces_ref[i])


def mates_kernel(partner_ref, pieces_ref, out_ref):
    for g in range(GROUPS):
        out_ref[g] = pieces_ref[partner_ref[g]]


def update_kernel(pieces_ref, delta_ref, weight_ref, momentum_ref, new_w_ref, new_m_ref, send_ref):
    rows = delta_ref.shape[0]
    for i in range(rows // SUB):
        at = slice(i * SUB, (i + 1) * SUB)
        average = 0.5 * (delta_ref[at] + pieces_ref[i].astype(f32))
        new_momentum = outer_beta * momentum_ref[at] + average
        new_weight = weight_ref[at] - outer_rate * (average + outer_beta * new_momentum)
        new_m_ref[at] = new_momentum
        new_w_ref[at] = new_weight
        for j in range(NFAR):
            send_ref[j, at] = new_weight.astype(bf16)


def cast_kernel(weight_ref, send_ref):
    for j in range(NFAR):
        send_ref[j] = weight_ref[...].astype(bf16)


def rollout_kernel(states_ref, mine_ref, other_ref, out_ref, full_ref):
    core = lax.axis_index("c")
    rows = mine_ref.shape[2]
    for far in range(NFAR):
        for near in range(NNEAR):
            full_ref[block_rows(far, near, core, rows), :] = mine_ref[near, far]
            full_ref[block_rows(far, near, 1 - core, rows), :] = other_ref[near, far]
    out = jnp.dot(states_ref[...], full_ref[...], preferred_element_type=f32) * scale
    out_ref[...] = out.astype(bf16)


def call(kernel, out, ins, scratch=(), name=None, mib=6):
    run = pl.pallas_call(
        kernel,
        out_shape=out,
        in_specs=[SMEM if space == "s" else VMEM for space in ins],
        out_specs=jax.tree.map(lambda _: VMEM, out),
        scratch_shapes=scratch,
        compiler_params=pltpu.CompilerParams(vmem_limit_bytes=mib << 20),
        name=name,
    )

    def apply(*args):
        held = [
            pltpu.with_memory_space_constraint(a, pltpu.MemorySpace.VMEM) if space == "v" else a
            for a, space in zip(args, ins)
        ]
        return run(*held)

    return apply


def gather_rows(send):
    far = lax.all_to_all(send, FAR, 0, 0)
    return lax.all_to_all(jnp.broadcast_to(far[None], (NNEAR,) + far.shape), NEAR, 0, 0)


def shards(weight, momentum, adam_mean, adam_var, inputs, targets, states, partner):
    weight, momentum, adam_mean, adam_var = weight[0], momentum[0], adam_mean[0], adam_var[0]
    inputs, targets, states, partner = inputs[0], targets[0], states[0], partner[:, 0]
    rows, width = weight.shape
    count, depth = inputs.shape
    tokens_all = count * NFAR * NNEAR * 2
    S = jax.ShapeDtypeStruct
    V = pltpu.VMEM

    inputs_other = lax.ppermute(inputs, "c", SWAP)
    send = call(cast_kernel, V((NFAR, rows, width), bf16), "h", name="cast")(weight)
    parts = gather_rows(send)
    here = call(
        pred_kernel, V((2, count, width), f32), "vvvv", [pltpu.VMEM((depth, width), bf16)], "pred", 16
    )(inputs, inputs_other, parts, targets)
    there = lax.ppermute(here, "c", SWAP)
    grads = call(
        functools.partial(grad_kernel, tokens_all),
        V((NNEAR, NFAR, rows, width), bf16),
        "vvvv",
        [pltpu.VMEM((NFAR, 2 * NNEAR * rows, width), f32)],
        "grad",
        20,
    )(inputs, inputs_other, here, there)
    near = lax.all_to_all(grads, NEAR, 0, 0)
    near = call(sum_kernel, V((NFAR, rows, width), bf16), "v", name="near_sum")(near)
    far = lax.all_to_all(near, FAR, 0, 0)
    piece = V((GROUPS, SUB, width), bf16)
    delta, pieces = call(delta_kernel, (V((rows, width), f32), piece), "vvvv", name="delta")(
        far, weight, adam_mean, adam_var
    )
    pieces = lax.all_to_all(pieces, GRP, 0, 0)
    pieces = call(mates_kernel, piece, "sv", name="mates")(partner, pieces)
    pieces = lax.all_to_all(pieces, GRP, 0, 0)
    new_weight, new_momentum, send = call(
        update_kernel,
        (S((rows, width), f32), S((rows, width), f32), V((NFAR, rows, width), bf16)),
        "vvvv",
        name="update",
    )(pieces, delta, weight, momentum)
    mine = gather_rows(send)
    other = lax.ppermute(mine, "c", SWAP)
    rollout = call(
        rollout_kernel,
        S((states.shape[0], width), bf16),
        "vvv",
        [pltpu.VMEM((depth, width), bf16)],
        "rollout",
        12,
    )(states, mine, other)
    return new_weight[None], new_momentum[None], rollout[None]


def solution(mesh):
    names = tuple(name for name, _ in AXES)
    fine = Mesh(mesh.devices.reshape(tuple(size for _, size in AXES)), names)
    row = P(GRP, FSDP, None)
    return jax.shard_map(
        shards,
        mesh=fine,
        in_specs=(row, row, row, row, row, row, row, P(None, FSDP)),
        out_specs=(row, row, row),
        check_vma=False,
    )
```

```python
import functools
import math

import jax
import jax.numpy as jnp
from jax import lax
from jax.experimental import pallas as pl
from jax.experimental.pallas import tpu as pltpu
from jax.sharding import Mesh
from jax.sharding import PartitionSpec as P

D = 4608

beta_one = 0.9
beta_two = 0.95
adam_eps = 1e-08
inner_rate = 0.1
decay_rate = 0.1
bias_one = 1.0 - (0.9**50) ** 2
bias_two = 1.0 - (0.95**50) ** 2
outer_rate = 0.7
outer_beta = 0.9
scale = 1.0 / math.sqrt(D)

f32, bf16 = jnp.float32, jnp.bfloat16

AXES = (("xl", 2), ("z", 8), ("yh", 4), ("yl", 2), ("xh", 2), ("c", 2))
GRP = ("xl", "z")
FSDP = ("yh", "yl", "xh", "c")
FAR = ("yh",)
NFAR, NNEAR = 4, 4
GROUPS = 16
SUB = 16
SWAP = [(0, 1), (1, 0)]

VMEM = pl.BlockSpec(memory_space=pltpu.MemorySpace.VMEM)
SMEM = pl.BlockSpec(memory_space=pltpu.MemorySpace.SMEM)


def block_rows(far, near, core, rows):
    pair, xh = near // 2, near % 2
    yl = core if pair == 0 else 1 - core
    start = rows * (2 * NNEAR * far + 2 * xh) + rows * core + 4 * rows * yl
    return pl.ds(pl.multiple_of(start, 16), rows)


def near_groups():
    groups = []
    for core in range(2):
        for k in range(4):
            ys = [(2 * k + core + i) % 8 for i in range(2)]
            groups.append([(y * 2 + xh) * 2 + core for y in ys for xh in range(2)])
    return groups


def pred_kernel(mine_ref, other_ref, weight_ref, target_ref, out_ref, full_ref):
    core = lax.axis_index("c")
    rows = weight_ref.shape[2]
    for far in range(NFAR):
        for near in range(NNEAR):
            full_ref[block_rows(far, near, core, rows), :] = weight_ref[near, far]
            full_ref[block_rows(far, near, 1 - core, rows), :] = jnp.zeros_like(weight_ref[near, far])
    mine = jnp.dot(mine_ref[...], full_ref[...], preferred_element_type=f32)
    out_ref[0] = mine * scale - target_ref[...].astype(f32)
    other = jnp.dot(other_ref[...], full_ref[...], preferred_element_type=f32)
    out_ref[1] = other * scale


def grad_kernel(tokens, mine_ref, other_ref, here_ref, there_ref, out_ref, part_ref):
    core = lax.axis_index("c")
    rows = out_ref.shape[2]
    resid_mine = ((here_ref[0] + there_ref[1]) / tokens).astype(bf16)
    resid_other = ((here_ref[1] + there_ref[0]) / tokens).astype(bf16)
    dims = (((0,), (0,)), ((), ()))
    span = 2 * NNEAR * rows
    for far in range(NFAR):
        cols = pl.ds(far * span, span)
        part_ref[far] = lax.dot_general(
            mine_ref[:, cols], resid_mine, dims, preferred_element_type=f32
        ) + lax.dot_general(other_ref[:, cols], resid_other, dims, preferred_element_type=f32)
        for near in range(NNEAR):
            out_ref[near, far] = part_ref[far, block_rows(0, near, core, rows), :].astype(bf16)


def sum_kernel(parts_ref, out_ref):
    total = parts_ref[0].astype(f32)
    for i in range(1, NNEAR):
        total += parts_ref[i].astype(f32)
    out_ref[...] = total.astype(bf16)


def delta_kernel(parts_ref, weight_ref, mean_ref, var_ref, delta_ref, pieces_ref):
    total = parts_ref[0].astype(f32)
    for i in range(1, NFAR):
        total += parts_ref[i].astype(f32)
    grad = total * scale
    mean_new = beta_one * mean_ref[...] + (1.0 - beta_one) * grad
    var_new = beta_two * var_ref[...] + (1.0 - beta_two) * grad * grad
    update = mean_new / bias_one / (jnp.sqrt(var_new / bias_two) + adam_eps)
    delta = inner_rate * (update + decay_rate * weight_ref[...])
    delta_ref[...] = delta
    rows = delta.shape[0]
    for i in range(GROUPS):
        if (i + 1) * SUB <= rows:
            pieces_ref[i] = delta[i * SUB : (i + 1) * SUB].astype(bf16)
        else:
            pieces_ref[i] = jnp.zeros_like(pieces_ref[i])


def mates_kernel(partner_ref, pieces_ref, out_ref):
    for g in range(GROUPS):
        out_ref[g] = pieces_ref[partner_ref[g]]


def update_kernel(pieces_ref, delta_ref, weight_ref, momentum_ref, new_w_ref, new_m_ref, send_ref):
    rows = delta_ref.shape[0]
    for i in range(rows // SUB):
        at = slice(i * SUB, (i + 1) * SUB)
        average = 0.5 * (delta_ref[at] + pieces_ref[i].astype(f32))
        new_momentum = outer_beta * momentum_ref[at] + average
        new_weight = weight_ref[at] - outer_rate * (average + outer_beta * new_momentum)
        new_m_ref[at] = new_momentum
        new_w_ref[at] = new_weight
        for j in range(NFAR):
            send_ref[j, at] = new_weight.astype(bf16)


def cast_kernel(weight_ref, send_ref):
    for j in range(NFAR):
        send_ref[j] = weight_ref[...].astype(bf16)


def rollout_kernel(states_ref, mine_ref, other_ref, out_ref, full_ref):
    core = lax.axis_index("c")
    rows = mine_ref.shape[2]
    for far in range(NFAR):
        for near in range(NNEAR):
            full_ref[block_rows(far, near, core, rows), :] = mine_ref[near, far]
            full_ref[block_rows(far, near, 1 - core, rows), :] = other_ref[near, far]
    out = jnp.dot(states_ref[...], full_ref[...], preferred_element_type=f32) * scale
    out_ref[...] = out.astype(bf16)


def call(kernel, out, ins, scratch=(), name=None, mib=6):
    run = pl.pallas_call(
        kernel,
        out_shape=out,
        in_specs=[SMEM if space == "s" else VMEM for space in ins],
        out_specs=jax.tree.map(lambda _: VMEM, out),
        scratch_shapes=scratch,
        compiler_params=pltpu.CompilerParams(vmem_limit_bytes=mib << 20),
        name=name,
    )

    def apply(*args):
        held = [
            pltpu.with_memory_space_constraint(a, pltpu.MemorySpace.VMEM) if space == "v" else a
            for a, space in zip(args, ins)
        ]
        return run(*held)

    return apply


def near_exchange(x):
    return lax.all_to_all(x, FSDP, 0, 0, axis_index_groups=near_groups())


def gather_rows(send):
    far = lax.all_to_all(send, FAR, 0, 0)
    return near_exchange(jnp.broadcast_to(far[None], (NNEAR,) + far.shape))


def shards(weight, momentum, adam_mean, adam_var, inputs, targets, states, partner):
    weight, momentum, adam_mean, adam_var = weight[0], momentum[0], adam_mean[0], adam_var[0]
    inputs, targets, states, partner = inputs[0], targets[0], states[0], partner[:, 0]
    rows, width = weight.shape
    count, depth = inputs.shape
    tokens_all = count * NFAR * NNEAR * 2
    S = jax.ShapeDtypeStruct
    V = pltpu.VMEM

    inputs_other = lax.ppermute(inputs, "c", SWAP)
    send = call(cast_kernel, V((NFAR, rows, width), bf16), "h", name="cast")(weight)
    parts = gather_rows(send)
    here = call(
        pred_kernel, V((2, count, width), f32), "vvvv", [pltpu.VMEM((depth, width), bf16)], "pred", 16
    )(inputs, inputs_other, parts, targets)
    there = lax.ppermute(here, "c", SWAP)
    grads = call(
        functools.partial(grad_kernel, tokens_all),
        V((NNEAR, NFAR, rows, width), bf16),
        "vvvv",
        [pltpu.VMEM((NFAR, 2 * NNEAR * rows, width), f32)],
        "grad",
        20,
    )(inputs, inputs_other, here, there)
    near = near_exchange(grads)
    near = call(sum_kernel, V((NFAR, rows, width), bf16), "v", name="near_sum")(near)
    far = lax.all_to_all(near, FAR, 0, 0)
    piece = V((GROUPS, SUB, width), bf16)
    delta, pieces = call(delta_kernel, (V((rows, width), f32), piece), "vvvv", name="delta")(
        far, weight, adam_mean, adam_var
    )
    pieces = lax.all_to_all(pieces, GRP, 0, 0)
    pieces = call(mates_kernel, piece, "sv", name="mates")(partner, pieces)
    pieces = lax.all_to_all(pieces, GRP, 0, 0)
    new_weight, new_momentum, send = call(
        update_kernel,
        (S((rows, width), f32), S((rows, width), f32), V((NFAR, rows, width), bf16)),
        "vvvv",
        name="update",
    )(pieces, delta, weight, momentum)
    mine = gather_rows(send)
    other = lax.ppermute(mine, "c", SWAP)
    rollout = call(
        rollout_kernel,
        S((states.shape[0], width), bf16),
        "vvv",
        [pltpu.VMEM((depth, width), bf16)],
        "rollout",
        12,
    )(states, mine, other)
    return new_weight[None], new_momentum[None], rollout[None]


def solution(mesh):
    names = tuple(name for name, _ in AXES)
    fine = Mesh(mesh.devices.reshape(tuple(size for _, size in AXES)), names)
    row = P(GRP, FSDP, None)
    return jax.shard_map(
        shards,
        mesh=fine,
        in_specs=(row, row, row, row, row, row, row, P(None, FSDP)),
        out_specs=(row, row, row),
        check_vma=False,
    )
```

```python
import functools
import math

import jax
import jax.numpy as jnp
from jax import lax
from jax.experimental import pallas as pl
from jax.experimental.pallas import tpu as pltpu
from jax.sharding import Mesh
from jax.sharding import PartitionSpec as P

D = 4608

beta_one = 0.9
beta_two = 0.95
adam_eps = 1e-08
inner_rate = 0.1
decay_rate = 0.1
bias_one = 1.0 - (0.9**50) ** 2
bias_two = 1.0 - (0.95**50) ** 2
outer_rate = 0.7
outer_beta = 0.9
scale = 1.0 / math.sqrt(D)

f32, bf16 = jnp.float32, jnp.bfloat16

AXES = (("xl", 2), ("z", 8), ("yh", 4), ("yl", 2), ("xh", 2), ("c", 2))
GRP = ("xl", "z")
FSDP = ("yh", "yl", "xh", "c")
FAR = ("yh",)
NEAR = ("yl", "xh")
NFAR, NNEAR = 4, 4
GROUPS = 16
SUB = 16
SWAP = [(0, 1), (1, 0)]

VMEM = pl.BlockSpec(memory_space=pltpu.MemorySpace.VMEM)
SMEM = pl.BlockSpec(memory_space=pltpu.MemorySpace.SMEM)


def block_rows(far, near, core, rows):
    start = rows * (2 * NNEAR * far + 2 * near) + rows * core
    return pl.ds(pl.multiple_of(start, 16), rows)


def pred_kernel(mine_ref, other_ref, weight_ref, target_ref, out_ref, full_ref):
    core = lax.axis_index("c")
    rows = weight_ref.shape[2]
    for far in range(NFAR):
        for near in range(NNEAR):
            full_ref[block_rows(far, near, core, rows), :] = weight_ref[near, far]
            full_ref[block_rows(far, near, 1 - core, rows), :] = jnp.zeros_like(weight_ref[near, far])
    mine = jnp.dot(mine_ref[...], full_ref[...], preferred_element_type=f32)
    out_ref[0] = mine * scale - target_ref[...].astype(f32)
    other = jnp.dot(other_ref[...], full_ref[...], preferred_element_type=f32)
    out_ref[1] = other * scale


def grad_kernel(tokens, mine_ref, other_ref, here_ref, there_ref, out_ref, part_ref):
    core = lax.axis_index("c")
    rows = out_ref.shape[2]
    resid_mine = ((here_ref[0] + there_ref[1]) / tokens).astype(bf16)
    resid_other = ((here_ref[1] + there_ref[0]) / tokens).astype(bf16)
    dims = (((0,), (0,)), ((), ()))
    span = 2 * NNEAR * rows
    for far in range(NFAR):
        cols = pl.ds(far * span, span)
        part_ref[far] = lax.dot_general(
            mine_ref[:, cols], resid_mine, dims, preferred_element_type=f32
        ) + lax.dot_general(other_ref[:, cols], resid_other, dims, preferred_element_type=f32)
        for near in range(NNEAR):
            out_ref[near, far] = part_ref[far, block_rows(0, near, core, rows), :].astype(bf16)


def sum_kernel(parts_ref, out_ref):
    total = parts_ref[0].astype(f32)
    for i in range(1, NNEAR):
        total += parts_ref[i].astype(f32)
    out_ref[...] = total.astype(bf16)


def delta_kernel(parts_ref, weight_ref, mean_ref, var_ref, delta_ref, pieces_ref):
    total = parts_ref[0].astype(f32)
    for i in range(1, NFAR):
        total += parts_ref[i].astype(f32)
    grad = total * scale
    mean_new = beta_one * mean_ref[...] + (1.0 - beta_one) * grad
    var_new = beta_two * var_ref[...] + (1.0 - beta_two) * grad * grad
    update = mean_new / bias_one / (jnp.sqrt(var_new / bias_two) + adam_eps)
    delta = inner_rate * (update + decay_rate * weight_ref[...])
    delta_ref[...] = delta
    rows = delta.shape[0]
    for i in range(GROUPS):
        if (i + 1) * SUB <= rows:
            pieces_ref[i] = delta[i * SUB : (i + 1) * SUB].astype(bf16)
        else:
            pieces_ref[i] = jnp.zeros_like(pieces_ref[i])


def mates_kernel(partner_ref, pieces_ref, out_ref):
    for g in range(GROUPS):
        out_ref[g] = pieces_ref[partner_ref[g]]


def update_kernel(pieces_ref, delta_ref, weight_ref, momentum_ref, new_w_ref, new_m_ref, send_ref):
    rows = delta_ref.shape[0]
    for i in range(rows // SUB):
        at = slice(i * SUB, (i + 1) * SUB)
        average = 0.5 * (delta_ref[at] + pieces_ref[i].astype(f32))
        new_momentum = outer_beta * momentum_ref[at] + average
        new_weight = weight_ref[at] - outer_rate * (average + outer_beta * new_momentum)
        new_m_ref[at] = new_momentum
        new_w_ref[at] = new_weight
        for j in range(NFAR):
            send_ref[j, at] = new_weight.astype(bf16)


def cast_kernel(weight_ref, send_ref):
    for j in range(NFAR):
        send_ref[j] = weight_ref[...].astype(bf16)


def place_kernel(mine_ref, full_ref):
    core = lax.axis_index("c")
    rows = mine_ref.shape[2]
    for far in range(NFAR):
        for near in range(NNEAR):
            full_ref[block_rows(far, near, core, rows), :] = mine_ref[near, far]


def rollout_kernel(states_ref, other_ref, full_ref, out_ref, whole_ref):
    core = lax.axis_index("c")
    rows = other_ref.shape[2]
    for far in range(NFAR):
        for near in range(NNEAR):
            whole_ref[block_rows(far, near, 1 - core, rows), :] = other_ref[near, far]
    out = jnp.dot(states_ref[...], whole_ref[...], preferred_element_type=f32) * scale
    out_ref[...] = out.astype(bf16)


def call(kernel, out, ins, scratch=(), name=None, mib=6, alias=None):
    run = pl.pallas_call(
        kernel,
        out_shape=out,
        in_specs=[SMEM if space == "s" else VMEM for space in ins],
        out_specs=jax.tree.map(lambda _: VMEM, out),
        scratch_shapes=scratch,
        input_output_aliases=alias or {},
        compiler_params=pltpu.CompilerParams(vmem_limit_bytes=mib << 20),
        name=name,
    )

    def apply(*args):
        held = [
            pltpu.with_memory_space_constraint(a, pltpu.MemorySpace.VMEM) if space == "v" else a
            for a, space in zip(args, ins)
        ]
        return run(*held)

    return apply


def gather_rows(send):
    far = lax.all_to_all(send, FAR, 0, 0)
    return lax.all_to_all(jnp.broadcast_to(far[None], (NNEAR,) + far.shape), NEAR, 0, 0)


def shards(weight, momentum, adam_mean, adam_var, inputs, targets, states, partner):
    weight, momentum, adam_mean, adam_var = weight[0], momentum[0], adam_mean[0], adam_var[0]
    inputs, targets, states, partner = inputs[0], targets[0], states[0], partner[:, 0]
    rows, width = weight.shape
    count, depth = inputs.shape
    tokens_all = count * NFAR * NNEAR * 2
    S = jax.ShapeDtypeStruct
    V = pltpu.VMEM

    inputs_other = lax.ppermute(inputs, "c", SWAP)
    send = call(cast_kernel, V((NFAR, rows, width), bf16), "h", name="cast")(weight)
    parts = gather_rows(send)
    here = call(
        pred_kernel, V((2, count, width), f32), "vvvv", [pltpu.VMEM((depth, width), bf16)], "pred", 16
    )(inputs, inputs_other, parts, targets)
    there = lax.ppermute(here, "c", SWAP)
    grads = call(
        functools.partial(grad_kernel, tokens_all),
        V((NNEAR, NFAR, rows, width), bf16),
        "vvvv",
        [pltpu.VMEM((NFAR, 2 * NNEAR * rows, width), f32)],
        "grad",
        20,
    )(inputs, inputs_other, here, there)
    near = lax.all_to_all(grads, NEAR, 0, 0)
    near = call(sum_kernel, V((NFAR, rows, width), bf16), "v", name="near_sum")(near)
    far = lax.all_to_all(near, FAR, 0, 0)
    piece = V((GROUPS, SUB, width), bf16)
    delta, pieces = call(delta_kernel, (V((rows, width), f32), piece), "vvvv", name="delta")(
        far, weight, adam_mean, adam_var
    )
    pieces = lax.all_to_all(pieces, GRP, 0, 0)
    pieces = call(mates_kernel, piece, "sv", name="mates")(partner, pieces)
    pieces = lax.all_to_all(pieces, GRP, 0, 0)
    new_weight, new_momentum, send = call(
        update_kernel,
        (V((rows, width), f32), V((rows, width), f32), V((NFAR, rows, width), bf16)),
        "vvvv",
        name="update",
    )(pieces, delta, weight, momentum)
    mine = gather_rows(send)
    other = lax.ppermute(mine, "c", SWAP)
    full = call(place_kernel, V((depth, width), bf16), "v", name="place")(mine)
    rollout, _ = call(
        rollout_kernel,
        (S((states.shape[0], width), bf16), V((depth, width), bf16)),
        "vvv",
        name="rollout",
        mib=8,
        alias={2: 1},
    )(states, other, full)
    return new_weight[None], new_momentum[None], rollout[None]


def solution(mesh):
    names = tuple(name for name, _ in AXES)
    fine = Mesh(mesh.devices.reshape(tuple(size for _, size in AXES)), names)
    row = P(GRP, FSDP, None)
    return jax.shard_map(
        shards,
        mesh=fine,
        in_specs=(row, row, row, row, row, row, row, P(None, FSDP)),
        out_specs=(row, row, row),
        check_vma=False,
    )
```

```python
import functools
import math

import jax
import jax.numpy as jnp
from jax import lax
from jax.experimental import pallas as pl
from jax.experimental.pallas import tpu as pltpu
from jax.sharding import Mesh
from jax.sharding import PartitionSpec as P

D = 4608

beta_one = 0.9
beta_two = 0.95
adam_eps = 1e-08
inner_rate = 0.1
decay_rate = 0.1
bias_one = 1.0 - (0.9**50) ** 2
bias_two = 1.0 - (0.95**50) ** 2
outer_rate = 0.7
outer_beta = 0.9
scale = 1.0 / math.sqrt(D)

f32, bf16 = jnp.float32, jnp.bfloat16

AXES = (("xl", 2), ("z", 8), ("yh", 4), ("yl", 2), ("xh", 2), ("c", 2))
GRP = ("xl", "z")
FSDP = ("yh", "yl", "xh", "c")
FAR = ("yh",)
NEAR = ("yl", "xh")
NFAR, NNEAR = 4, 4
GROUPS = 16
SUB = 16
SWAP = [(0, 1), (1, 0)]

VMEM = pl.BlockSpec(memory_space=pltpu.MemorySpace.VMEM)
SMEM = pl.BlockSpec(memory_space=pltpu.MemorySpace.SMEM)


def block_rows(far, near, core, rows):
    start = rows * (2 * NNEAR * far + 2 * near) + rows * core
    return pl.ds(pl.multiple_of(start, 16), rows)


def pred_kernel(mine_ref, other_ref, weight_ref, target_ref, out_ref, send_ref, full_ref):
    core = lax.axis_index("c")
    rows = weight_ref.shape[2]
    for far in range(NFAR):
        for near in range(NNEAR):
            full_ref[block_rows(far, near, core, rows), :] = weight_ref[near, far]
            full_ref[block_rows(far, near, 1 - core, rows), :] = jnp.zeros_like(weight_ref[near, far])
    mine = jnp.dot(mine_ref[...], full_ref[...], preferred_element_type=f32)
    mine = mine * scale - target_ref[...].astype(f32)
    out_ref[0] = mine
    send_ref[0] = mine.astype(bf16)
    other = jnp.dot(other_ref[...], full_ref[...], preferred_element_type=f32)
    other = other * scale
    out_ref[1] = other
    send_ref[1] = other.astype(bf16)


def grad_kernel(tokens, mine_ref, other_ref, here_ref, there_ref, out_ref, part_ref):
    core = lax.axis_index("c")
    rows = out_ref.shape[2]
    resid_mine = ((here_ref[0] + there_ref[1].astype(f32)) / tokens).astype(bf16)
    resid_other = ((here_ref[1] + there_ref[0].astype(f32)) / tokens).astype(bf16)
    dims = (((0,), (0,)), ((), ()))
    span = 2 * NNEAR * rows
    for far in range(NFAR):
        cols = pl.ds(far * span, span)
        part_ref[far] = lax.dot_general(
            mine_ref[:, cols], resid_mine, dims, preferred_element_type=f32
        ) + lax.dot_general(other_ref[:, cols], resid_other, dims, preferred_element_type=f32)
        for near in range(NNEAR):
            out_ref[near, far] = part_ref[far, block_rows(0, near, core, rows), :].astype(bf16)


def sum_kernel(parts_ref, out_ref):
    total = parts_ref[0].astype(f32)
    for i in range(1, NNEAR):
        total += parts_ref[i].astype(f32)
    out_ref[...] = total.astype(bf16)


def delta_kernel(parts_ref, weight_ref, mean_ref, var_ref, delta_ref, pieces_ref):
    total = parts_ref[0].astype(f32)
    for i in range(1, NFAR):
        total += parts_ref[i].astype(f32)
    grad = total * scale
    mean_new = beta_one * mean_ref[...] + (1.0 - beta_one) * grad
    var_new = beta_two * var_ref[...] + (1.0 - beta_two) * grad * grad
    update = mean_new / bias_one / (jnp.sqrt(var_new / bias_two) + adam_eps)
    delta = inner_rate * (update + decay_rate * weight_ref[...])
    delta_ref[...] = delta
    rows = delta.shape[0]
    for i in range(GROUPS):
        if (i + 1) * SUB <= rows:
            pieces_ref[i] = delta[i * SUB : (i + 1) * SUB].astype(bf16)
        else:
            pieces_ref[i] = jnp.zeros_like(pieces_ref[i])


def mates_kernel(partner_ref, pieces_ref, out_ref):
    for g in range(GROUPS):
        out_ref[g] = pieces_ref[partner_ref[g]]


def update_kernel(pieces_ref, delta_ref, weight_ref, momentum_ref, new_w_ref, new_m_ref, send_ref):
    rows = delta_ref.shape[0]
    for i in range(rows // SUB):
        at = slice(i * SUB, (i + 1) * SUB)
        average = 0.5 * (delta_ref[at] + pieces_ref[i].astype(f32))
        new_momentum = outer_beta * momentum_ref[at] + average
        new_weight = weight_ref[at] - outer_rate * (average + outer_beta * new_momentum)
        new_m_ref[at] = new_momentum
        new_w_ref[at] = new_weight
        for j in range(NFAR):
            send_ref[j, at] = new_weight.astype(bf16)


def cast_kernel(weight_ref, send_ref):
    for j in range(NFAR):
        send_ref[j] = weight_ref[...].astype(bf16)


def place_kernel(mine_ref, full_ref):
    core = lax.axis_index("c")
    rows = mine_ref.shape[2]
    for far in range(NFAR):
        for near in range(NNEAR):
            full_ref[block_rows(far, near, core, rows), :] = mine_ref[near, far]


def rollout_kernel(states_ref, other_ref, full_ref, out_ref, whole_ref):
    core = lax.axis_index("c")
    rows = other_ref.shape[2]
    for far in range(NFAR):
        for near in range(NNEAR):
            whole_ref[block_rows(far, near, 1 - core, rows), :] = other_ref[near, far]
    out = jnp.dot(states_ref[...], whole_ref[...], preferred_element_type=f32) * scale
    out_ref[...] = out.astype(bf16)


def call(kernel, out, ins, scratch=(), name=None, mib=6, alias=None):
    run = pl.pallas_call(
        kernel,
        out_shape=out,
        in_specs=[SMEM if space == "s" else VMEM for space in ins],
        out_specs=jax.tree.map(lambda _: VMEM, out),
        scratch_shapes=scratch,
        input_output_aliases=alias or {},
        compiler_params=pltpu.CompilerParams(vmem_limit_bytes=mib << 20),
        name=name,
    )

    def apply(*args):
        held = [
            pltpu.with_memory_space_constraint(a, pltpu.MemorySpace.VMEM) if space == "v" else a
            for a, space in zip(args, ins)
        ]
        return run(*held)

    return apply


def gather_rows(send):
    far = lax.all_to_all(send, FAR, 0, 0)
    return lax.all_to_all(jnp.broadcast_to(far[None], (NNEAR,) + far.shape), NEAR, 0, 0)


def shards(weight, momentum, adam_mean, adam_var, inputs, targets, states, partner):
    weight, momentum, adam_mean, adam_var = weight[0], momentum[0], adam_mean[0], adam_var[0]
    inputs, targets, states, partner = inputs[0], targets[0], states[0], partner[:, 0]
    rows, width = weight.shape
    count, depth = inputs.shape
    tokens_all = count * NFAR * NNEAR * 2
    S = jax.ShapeDtypeStruct
    V = pltpu.VMEM

    inputs_other = lax.ppermute(inputs, "c", SWAP)
    send = call(cast_kernel, V((NFAR, rows, width), bf16), "h", name="cast")(weight)
    parts = gather_rows(send)
    shape = (2, count, width)
    here, sent = call(
        pred_kernel, (V(shape, f32), V(shape, bf16)), "vvvv", [pltpu.VMEM((depth, width), bf16)], "pred", 16
    )(inputs, inputs_other, parts, targets)
    there = lax.ppermute(sent, "c", SWAP)
    grads = call(
        functools.partial(grad_kernel, tokens_all),
        V((NNEAR, NFAR, rows, width), bf16),
        "vvvv",
        [pltpu.VMEM((NFAR, 2 * NNEAR * rows, width), f32)],
        "grad",
        20,
    )(inputs, inputs_other, here, there)
    near = lax.all_to_all(grads, NEAR, 0, 0)
    near = call(sum_kernel, V((NFAR, rows, width), bf16), "v", name="near_sum")(near)
    far = lax.all_to_all(near, FAR, 0, 0)
    piece = V((GROUPS, SUB, width), bf16)
    delta, pieces = call(delta_kernel, (V((rows, width), f32), piece), "vvvv", name="delta")(
        far, weight, adam_mean, adam_var
    )
    pieces = lax.all_to_all(pieces, GRP, 0, 0)
    pieces = call(mates_kernel, piece, "sv", name="mates")(partner, pieces)
    pieces = lax.all_to_all(pieces, GRP, 0, 0)
    new_weight, new_momentum, send = call(
        update_kernel,
        (V((rows, width), f32), V((rows, width), f32), V((NFAR, rows, width), bf16)),
        "vvvv",
        name="update",
    )(pieces, delta, weight, momentum)
    mine = gather_rows(send)
    other = lax.ppermute(mine, "c", SWAP)
    full = call(place_kernel, V((depth, width), bf16), "v", name="place")(mine)
    rollout, _ = call(
        rollout_kernel,
        (S((states.shape[0], width), bf16), V((depth, width), bf16)),
        "vvv",
        name="rollout",
        mib=8,
        alias={2: 1},
    )(states, other, full)
    return new_weight[None], new_momentum[None], rollout[None]


def solution(mesh):
    names = tuple(name for name, _ in AXES)
    fine = Mesh(mesh.devices.reshape(tuple(size for _, size in AXES)), names)
    row = P(GRP, FSDP, None)
    return jax.shard_map(
        shards,
        mesh=fine,
        in_specs=(row, row, row, row, row, row, row, P(None, FSDP)),
        out_specs=(row, row, row),
        check_vma=False,
    )
```

```python
import functools
import math

import jax
import jax.numpy as jnp
from jax import lax
from jax.experimental import pallas as pl
from jax.experimental.pallas import tpu as pltpu
from jax.sharding import Mesh
from jax.sharding import PartitionSpec as P

D = 4608

beta_one = 0.9
beta_two = 0.95
adam_eps = 1e-08
inner_rate = 0.1
decay_rate = 0.1
bias_one = 1.0 - (0.9**50) ** 2
bias_two = 1.0 - (0.95**50) ** 2
outer_rate = 0.7
outer_beta = 0.9
scale = 1.0 / math.sqrt(D)

f32, bf16 = jnp.float32, jnp.bfloat16

AXES = (("xl", 2), ("z", 8), ("yh", 4), ("yl", 2), ("xh", 2), ("c", 2))
GRP = ("xl", "z")
FSDP = ("yh", "yl", "xh", "c")
FAR = ("yh",)
NEAR = ("yl", "xh")
NFAR, NNEAR = 4, 4
GROUPS = 16
SUB = 16
SWAP = [(0, 1), (1, 0)]

VMEM = pl.BlockSpec(memory_space=pltpu.MemorySpace.VMEM)
SMEM = pl.BlockSpec(memory_space=pltpu.MemorySpace.SMEM)


def block_rows(far, near, core, rows):
    start = rows * (2 * NNEAR * far + 2 * near) + rows * core
    return pl.ds(pl.multiple_of(start, 16), rows)


def pred_kernel(mine_ref, other_ref, weight_ref, target_ref, out_ref, send_ref, full_ref):
    core = lax.axis_index("c")
    rows = weight_ref.shape[2]
    for far in range(NFAR):
        for near in range(NNEAR):
            full_ref[block_rows(far, near, core, rows), :] = weight_ref[near, far]
            full_ref[block_rows(far, near, 1 - core, rows), :] = jnp.zeros_like(weight_ref[near, far])
    mine = jnp.dot(mine_ref[...], full_ref[...], preferred_element_type=f32)
    mine = mine * scale - target_ref[...].astype(f32)
    out_ref[0] = mine
    send_ref[0] = mine.astype(bf16)
    other = jnp.dot(other_ref[...], full_ref[...], preferred_element_type=f32)
    other = other * scale
    out_ref[1] = other
    send_ref[1] = other.astype(bf16)


def grad_kernel(tokens, mine_ref, other_ref, here_ref, there_ref, out_ref, part_ref):
    core = lax.axis_index("c")
    rows = out_ref.shape[2]
    resid_mine = ((here_ref[0] + there_ref[1].astype(f32)) / tokens).astype(bf16)
    resid_other = ((here_ref[1] + there_ref[0].astype(f32)) / tokens).astype(bf16)
    dims = (((0,), (0,)), ((), ()))
    span = 2 * NNEAR * rows
    for far in range(NFAR):
        cols = pl.ds(far * span, span)
        part_ref[far] = jnp.dot(
            mine_ref[cols, :], resid_mine, preferred_element_type=f32
        ) + lax.dot_general(other_ref[:, cols], resid_other, dims, preferred_element_type=f32)
        for near in range(NNEAR):
            out_ref[near, far] = part_ref[far, block_rows(0, near, core, rows), :].astype(bf16)


def turn_kernel(tokens_ref, out_ref):
    out_ref[...] = tokens_ref[...].T


def sum_kernel(parts_ref, out_ref):
    total = parts_ref[0].astype(f32)
    for i in range(1, NNEAR):
        total += parts_ref[i].astype(f32)
    out_ref[...] = total.astype(bf16)


def delta_kernel(parts_ref, weight_ref, mean_ref, var_ref, delta_ref, pieces_ref):
    total = parts_ref[0].astype(f32)
    for i in range(1, NFAR):
        total += parts_ref[i].astype(f32)
    grad = total * scale
    mean_new = beta_one * mean_ref[...] + (1.0 - beta_one) * grad
    var_new = beta_two * var_ref[...] + (1.0 - beta_two) * grad * grad
    update = mean_new / bias_one / (jnp.sqrt(var_new / bias_two) + adam_eps)
    delta = inner_rate * (update + decay_rate * weight_ref[...])
    delta_ref[...] = delta
    rows = delta.shape[0]
    for i in range(GROUPS):
        if (i + 1) * SUB <= rows:
            pieces_ref[i] = delta[i * SUB : (i + 1) * SUB].astype(bf16)
        else:
            pieces_ref[i] = jnp.zeros_like(pieces_ref[i])


def mates_kernel(partner_ref, pieces_ref, out_ref):
    for g in range(GROUPS):
        out_ref[g] = pieces_ref[partner_ref[g]]


def update_kernel(pieces_ref, delta_ref, weight_ref, momentum_ref, new_w_ref, new_m_ref, send_ref):
    rows = delta_ref.shape[0]
    for i in range(rows // SUB):
        at = slice(i * SUB, (i + 1) * SUB)
        average = 0.5 * (delta_ref[at] + pieces_ref[i].astype(f32))
        new_momentum = outer_beta * momentum_ref[at] + average
        new_weight = weight_ref[at] - outer_rate * (average + outer_beta * new_momentum)
        new_m_ref[at] = new_momentum
        new_w_ref[at] = new_weight
        for j in range(NFAR):
            send_ref[j, at] = new_weight.astype(bf16)


def cast_kernel(weight_ref, send_ref):
    for j in range(NFAR):
        send_ref[j] = weight_ref[...].astype(bf16)


def place_kernel(mine_ref, full_ref):
    core = lax.axis_index("c")
    rows = mine_ref.shape[2]
    for far in range(NFAR):
        for near in range(NNEAR):
            full_ref[block_rows(far, near, core, rows), :] = mine_ref[near, far]


def rollout_kernel(states_ref, other_ref, full_ref, out_ref, whole_ref):
    core = lax.axis_index("c")
    rows = other_ref.shape[2]
    for far in range(NFAR):
        for near in range(NNEAR):
            whole_ref[block_rows(far, near, 1 - core, rows), :] = other_ref[near, far]
    out = jnp.dot(states_ref[...], whole_ref[...], preferred_element_type=f32) * scale
    out_ref[...] = out.astype(bf16)


def call(kernel, out, ins, scratch=(), name=None, mib=6, alias=None):
    run = pl.pallas_call(
        kernel,
        out_shape=out,
        in_specs=[SMEM if space == "s" else VMEM for space in ins],
        out_specs=jax.tree.map(lambda _: VMEM, out),
        scratch_shapes=scratch,
        input_output_aliases=alias or {},
        compiler_params=pltpu.CompilerParams(vmem_limit_bytes=mib << 20),
        name=name,
    )

    def apply(*args):
        held = [
            pltpu.with_memory_space_constraint(a, pltpu.MemorySpace.VMEM) if space == "v" else a
            for a, space in zip(args, ins)
        ]
        return run(*held)

    return apply


def gather_rows(send):
    far = lax.all_to_all(send, FAR, 0, 0)
    return lax.all_to_all(jnp.broadcast_to(far[None], (NNEAR,) + far.shape), NEAR, 0, 0)


def shards(weight, momentum, adam_mean, adam_var, inputs, targets, states, partner):
    weight, momentum, adam_mean, adam_var = weight[0], momentum[0], adam_mean[0], adam_var[0]
    inputs, targets, states, partner = inputs[0], targets[0], states[0], partner[:, 0]
    rows, width = weight.shape
    count, depth = inputs.shape
    tokens_all = count * NFAR * NNEAR * 2
    S = jax.ShapeDtypeStruct
    V = pltpu.VMEM

    inputs_other = lax.ppermute(inputs, "c", SWAP)
    send = call(cast_kernel, V((NFAR, rows, width), bf16), "h", name="cast")(weight)
    parts = gather_rows(send)
    shape = (2, count, width)
    here, sent = call(
        pred_kernel, (V(shape, f32), V(shape, bf16)), "vvvv", [pltpu.VMEM((depth, width), bf16)], "pred", 16
    )(inputs, inputs_other, parts, targets)
    there = lax.ppermute(sent, "c", SWAP)
    held, here = lax.optimization_barrier((inputs, here))
    turned = call(turn_kernel, V((depth, count), bf16), "v", name="turn", mib=8)(held)
    grads = call(
        functools.partial(grad_kernel, tokens_all),
        V((NNEAR, NFAR, rows, width), bf16),
        "vvvv",
        [pltpu.VMEM((NFAR, 2 * NNEAR * rows, width), f32)],
        "grad",
        20,
    )(turned, inputs_other, here, there)
    near = lax.all_to_all(grads, NEAR, 0, 0)
    near = call(sum_kernel, V((NFAR, rows, width), bf16), "v", name="near_sum")(near)
    far = lax.all_to_all(near, FAR, 0, 0)
    piece = V((GROUPS, SUB, width), bf16)
    delta, pieces = call(delta_kernel, (V((rows, width), f32), piece), "vvvv", name="delta")(
        far, weight, adam_mean, adam_var
    )
    pieces = lax.all_to_all(pieces, GRP, 0, 0)
    pieces = call(mates_kernel, piece, "sv", name="mates")(partner, pieces)
    pieces = lax.all_to_all(pieces, GRP, 0, 0)
    new_weight, new_momentum, send = call(
        update_kernel,
        (V((rows, width), f32), V((rows, width), f32), V((NFAR, rows, width), bf16)),
        "vvvv",
        name="update",
    )(pieces, delta, weight, momentum)
    mine = gather_rows(send)
    other = lax.ppermute(mine, "c", SWAP)
    full = call(place_kernel, V((depth, width), bf16), "v", name="place")(mine)
    rollout, _ = call(
        rollout_kernel,
        (S((states.shape[0], width), bf16), V((depth, width), bf16)),
        "vvv",
        name="rollout",
        mib=8,
        alias={2: 1},
    )(states, other, full)
    return new_weight[None], new_momentum[None], rollout[None]


def solution(mesh):
    names = tuple(name for name, _ in AXES)
    fine = Mesh(mesh.devices.reshape(tuple(size for _, size in AXES)), names)
    row = P(GRP, FSDP, None)
    return jax.shard_map(
        shards,
        mesh=fine,
        in_specs=(row, row, row, row, row, row, row, P(None, FSDP)),
        out_specs=(row, row, row),
        check_vma=False,
    )
```
